32 devices in a mesh: groups: 2 (over y), ep: 8 (over z, x), tp: 2 (over core).
Axes of the slice: x: 2, y: 2, z: 4, core: 2. Of those that a mesh axis runs over, the one named last changes fastest.
Arguments:
- hidden: bfloat16 [128, 4096], P(('groups', 'ep', 'tp')), parts along dimension 0, may hold values from -6 to 6
- norm_gain: float32 [4096], replicated, may hold values from 0.5 to 1.5
- rot_left: float32 [64, 64], replicated, may hold values from -0.75 to 0.75
- rot_right: float32 [64, 64], replicated, may hold values from -0.75 to 0.75
- expert_ids: int32 [128, 8], P(('groups', 'ep')), parts along dimension 0, may hold values from 0 to 63, as said below
- gate_weights: float32 [128, 8], P(('groups', 'ep')), parts along dimension 0, may hold values from 0.05 to 1
- w_gate: bfloat16 [128, 4096, 384], P('ep', 'tp'), may hold values from -0.09375 to 0.09375
- w_up: bfloat16 [128, 4096, 384], P('ep', 'tp'), may hold values from -0.09375 to 0.09375
- w_down: bfloat16 [128, 384, 4096], P('ep', None, 'tp'), may hold values from -0.21875 to 0.21875
- unit_scales: float32 [128, 2, 384], P('ep'), may hold values from 0.25 to 1.75
Outputs:
- moe_out: bfloat16 [128, 4096], P(('groups', 'ep', 'tp')), parts along dimension 0
The draws below stay inside these ranges and needn't reach their ends.
There are 2 independent parts, one for each index of `groups`. The reference program is written for one: setup_inputs(seed, part) draws one part's arguments, and reference() takes and returns one part's arrays. A program takes and returns all parts, laid end to end along the dimension named above; an argument that names none is the same for every part. Nothing has to cross between parts.
Inputs may be any that keep to these rules, and one draw needn't show every extreme that they name: `expert_ids`: each row names 8 different experts. In each aligned block of 8 rows (the rows of one index of ep) no expert is named by more than 2 rows, and in every block some experts are named by exactly 2 rows; every expert is named by exactly 2 rows in some block.
All inputs are finite; a program needn't handle non-finite values.
Results may differ from the reference program's by a relative error of at most 0.0082.
Values may be sent and summed in bfloat16 or wider, within the bound.
A program may use at most 128 MiB of HBM per device.

```python
import math
import jax
import jax.numpy as jnp
from jax import lax

D = 4096
ROT = 64
FF = 768
EXPERTS = 64
TOPK = 8
R_DEV = 4
ROWS = 64
CAP = 2
N_TP = 2


def draw_expert_ids(key, part):
    group_rows = R_DEV * N_TP
    block_count = ROWS // group_rows
    labels = jax.random.permutation(jax.random.fold_in(key, 11), EXPERTS).astype(jnp.int32)
    offset = jax.random.randint(jax.random.fold_in(key, 12), (), 0, EXPERTS, dtype=jnp.int32)
    block_index = jnp.arange(block_count, dtype=jnp.int32)[:, None, None]
    row_index = jnp.arange(group_rows, dtype=jnp.int32)[None, :, None]
    choice_index = jnp.arange(TOPK, dtype=jnp.int32)[None, None, :]
    spot = (block_index * TOPK + row_index // CAP * TOPK + choice_index + offset) % EXPERTS
    chosen = labels[spot]

    def order_of(block):
        return jax.random.permutation(jax.random.fold_in(key, 1000 + block), group_rows).astype(jnp.int32)
    orders = jax.vmap(order_of)(jnp.arange(block_count, dtype=jnp.int32))
    chosen = jnp.take_along_axis(chosen, orders[:, :, None], axis=1)
    return chosen.reshape(ROWS, TOPK).astype(jnp.int32)


def block_levels(stream_key, extent, shards, low, high):
    level = 1.0
    for dim, parts in shards:
        heights = jax.random.uniform(jax.random.fold_in(jax.random.fold_in(stream_key, 6), dim), (parts,), jnp.float32, low / len(shards), high / len(shards))
        level = level * jnp.repeat(jnp.exp(heights), extent[dim] // parts).reshape((-1,) + (1,) * (len(extent) - 1 - dim))
    return level


def gaussian(rng, shape, width, limit, shards=(), kind=jnp.bfloat16):
    entries = jax.random.normal(rng, shape, jnp.float32) * width
    if len(shards) > 0:
        entries = block_levels(rng, shape, shards, -0.22, 0.18) * entries
    return jnp.clip(entries, min=-limit, max=limit).astype(kind)


def setup_inputs(seed: int = 0, part: int = 0) -> dict:
    keys = jax.random.split(jax.random.key(seed), 11)
    part_splits = jax.random.split(jax.random.fold_in(keys[10], part), 11)
    hidden = gaussian(part_splits[0], (ROWS, D), 1.0, 6.0, ((0, 16),))
    norm_gain = jnp.clip(1.0 + 0.1 * jax.random.normal(keys[1], (D,), jnp.float32), 0.5, 1.5)
    rot_left = gaussian(keys[2], (ROT, ROT), ROT ** -0.5, 0.75, (), jnp.float32)
    rot_right = gaussian(keys[3], (ROT, ROT), ROT ** -0.5, 0.75, (), jnp.float32)
    expert_ids = draw_expert_ids(jax.random.fold_in(jax.random.fold_in(keys[10], part), 71), part)
    gate_weights = jnp.clip(jnp.exp(math.log(1.0) - 2.9957323 * jax.random.uniform(part_splits[5], (ROWS, TOPK), jnp.float32) ** block_levels(part_splits[5], (ROWS, TOPK), ((0, 8),), -0.2, 0.2)), 0.05, 1.0)
    w_gate = gaussian(keys[6], (2 * EXPERTS, D, FF // 2), D ** -0.5, 0.09375, ((0, 8), (1, 2)))
    w_up = gaussian(keys[7], (2 * EXPERTS, D, FF // 2), D ** -0.5, 0.09375, ((0, 8), (1, 2)))
    w_down = gaussian(keys[8], (2 * EXPERTS, FF // 2, D), FF ** -0.5, 0.21875, ((0, 8), (2, 2)))
    unit_scales = jnp.clip(1.0 + 0.15 * jax.random.normal(keys[9], (2 * EXPERTS, 2, FF // 2), jnp.float32), 0.25, 1.75)
    return {"hidden": hidden, "norm_gain": norm_gain, "rot_left": rot_left, "rot_right": rot_right, "expert_ids": expert_ids, "gate_weights": gate_weights, "w_gate": w_gate, "w_up": w_up, "w_down": w_down, "unit_scales": unit_scales}


def rotate(hidden, norm_gain, rot_left, rot_right):
    values = hidden.astype(jnp.float32)
    mean_square = lax.optimization_barrier(jnp.mean(values * values, axis=1, keepdims=True))
    normed = values * lax.rsqrt(mean_square + 1e-06) * norm_gain[None, :]
    factor = rot_left.shape[0]
    square = normed.reshape(-1, factor, factor)
    turned = jnp.einsum('ij,rjk->rik', rot_left, square, precision=lax.Precision.HIGHEST)
    turned = jnp.einsum('rik,lk->ril', turned, rot_right, precision=lax.Precision.HIGHEST)
    return turned.reshape(normed.shape).astype(jnp.bfloat16)

def reference(hidden, norm_gain, rot_left, rot_right, expert_ids, gate_weights, w_gate, w_up, w_down, unit_scales):
    row_count = hidden.shape[0]
    group_rows = R_DEV * N_TP
    block_count = row_count // group_rows
    half_ff = w_gate.shape[2]
    rotated = rotate(hidden, norm_gain, rot_left, rot_right)
    weight_norm = (gate_weights / lax.optimization_barrier(jnp.sum(gate_weights, axis=1, keepdims=True))).astype(jnp.bfloat16)
    blocks = expert_ids.reshape(block_count, group_rows * TOPK)
    onehot = (blocks[:, :, None] == jnp.arange(EXPERTS, dtype=jnp.int32)[None, None, :]).astype(jnp.int32)
    slot_rank = lax.optimization_barrier(jnp.sum((jnp.cumsum(onehot, axis=1) - onehot) * onehot, axis=2))
    position = (jnp.arange(block_count, dtype=jnp.int32)[:, None] * group_rows + jnp.arange(group_rows * TOPK, dtype=jnp.int32)[None, :] // TOPK).astype(jnp.int32)
    weight_flat = weight_norm.astype(jnp.float32).reshape(block_count, group_rows * TOPK)
    slot_index = jnp.arange(CAP, dtype=jnp.int32)

    def expert_step(total, expert):
        selects = ((blocks == expert)[:, :, None] & (slot_rank[:, :, None] == slot_index[None, None, :])).astype(jnp.int32)
        gather_index = lax.optimization_barrier(jnp.sum(selects * position[:, :, None], axis=1)).reshape(-1).astype(jnp.int32)
        portion = lax.optimization_barrier(jnp.sum(selects.astype(jnp.float32) * weight_flat[:, :, None], axis=1)).reshape(-1)
        inputs = jnp.take(rotated, gather_index, axis=0)
        gate_full = jnp.concatenate((w_gate[expert], w_gate[EXPERTS + expert]), axis=1)
        up_full = jnp.concatenate((w_up[expert], w_up[EXPERTS + expert]), axis=1)
        gate_scale = jnp.concatenate((unit_scales[expert, 0], unit_scales[EXPERTS + expert, 0]), axis=0)
        up_scale = jnp.concatenate((unit_scales[expert, 1], unit_scales[EXPERTS + expert, 1]), axis=0)
        gate_sum = jnp.dot(inputs, gate_full, preferred_element_type=jnp.float32) * gate_scale[None, :]
        up_sum = jnp.dot(inputs, up_full, preferred_element_type=jnp.float32) * up_scale[None, :]
        hidden_units = (jax.nn.silu(gate_sum) * up_sum).astype(jnp.bfloat16)
        lower_out = jnp.dot(hidden_units[:, :half_ff], w_down[expert], preferred_element_type=jnp.float32).astype(jnp.bfloat16)
        upper_out = jnp.dot(hidden_units[:, half_ff:], w_down[EXPERTS + expert], preferred_element_type=jnp.float32).astype(jnp.bfloat16)
        expert_out = lax.optimization_barrier((lower_out.astype(jnp.float32) + upper_out.astype(jnp.float32)).astype(jnp.bfloat16))
        contribution = portion[:, None] * expert_out.astype(jnp.float32)
        return (total.at[gather_index].add(contribution), None)
    start = jnp.zeros((row_count, hidden.shape[1]), jnp.float32)
    total, _ = lax.scan(expert_step, start, jnp.arange(EXPERTS, dtype=jnp.int32))
    return total.astype(jnp.bfloat16)
```

```python
import functools

import jax
import jax.numpy as jnp
from jax import lax
from jax.experimental import pallas as pl
from jax.experimental.pallas import tpu as pltpu
from jax.sharding import PartitionSpec as P

MESH = pl.DeviceIdType.MESH
HIGH = lax.Precision.HIGHEST
LANES = 128
SUBLANES = 8
PAIR = 2
LAG = 2
SPLIT = 2
UNIT_RING = 14
DOWN_RING = 9
EARLY = 2
GROUP = 4
CHUNKS = 4
UNROLL = 32


def iota(shape, dim):
    return lax.broadcasted_iota(jnp.int32, shape, dim)


def rotate(hid_ref, gain_ref, left_ref, right_ref, n_tp):
    values = hid_ref[...].astype(jnp.float32)
    rows, width = values.shape
    half = width // n_tp
    order = left_ref.shape[0]
    mean_square = jnp.mean(values * values, axis=1, keepdims=True)
    normed = values * lax.rsqrt(mean_square + 1e-06) * gain_ref[...]
    stacked = jnp.concatenate([normed[:, h * half : (h + 1) * half] for h in range(n_tp)], axis=0)
    groups = half // LANES
    tall = jnp.concatenate(
        [stacked[:, m * LANES : (m + 1) * LANES] for m in range(groups)], axis=0
    )
    per_lane = LANES // order
    tall = jnp.concatenate(
        [tall[:, p * order : (p + 1) * order] for p in range(per_lane)], axis=0
    )
    count = tall.shape[0]
    block = n_tp * rows

    def line_of(index):
        return (
            (index % block) // rows * (half // order)
            + index // block % groups * per_lane
            + index // (block * groups)
        )

    spread = (line_of(iota((count, order), 0)) == iota((count, order), 1)).astype(jnp.float32)
    dims = (((1,), (1,)), ((), ()))
    wide = lax.dot_general(
        jnp.dot(spread, left_ref[...], precision=HIGH, preferred_element_type=jnp.float32),
        spread,
        dims,
        precision=HIGH,
        preferred_element_type=jnp.float32,
    )
    same_row = iota((count, count), 0) % rows == iota((count, count), 1) % rows
    wide = jnp.where(same_row, wide, 0.0)
    turned = lax.dot_general(
        tall, right_ref[...], dims, precision=HIGH, preferred_element_type=jnp.float32
    )
    turned = jnp.dot(wide, turned, precision=HIGH, preferred_element_type=jnp.float32)
    step = count // per_lane
    flat = jnp.concatenate([turned[p * step : (p + 1) * step] for p in range(per_lane)], axis=1)
    return jnp.concatenate([flat[m * block : (m + 1) * block] for m in range(groups)], axis=1)


def routing(ids_ref, weights_ref, experts, capacity):
    ids = ids_ref[...]
    weights = weights_ref[...]
    rows, choices = ids.shape
    weights = weights / jnp.sum(weights, axis=1, keepdims=True)
    weights = weights.astype(jnp.bfloat16).astype(jnp.float32)
    lane = iota((rows, capacity * experts), 1)
    expert = lane % experts
    named = jnp.zeros(lane.shape, jnp.float32)
    value = jnp.zeros(lane.shape, jnp.float32)
    for k in range(choices):
        hit = (ids[:, k : k + 1] == expert).astype(jnp.float32)
        named = named + hit
        value = value + hit * weights[:, k : k + 1]
    row = iota(lane.shape, 0)
    rank = jnp.zeros(lane.shape, jnp.float32)
    for r in range(rows):
        rank = rank + jnp.where(row > r, named[r : r + 1, :], 0.0)
    return jnp.where(rank == (lane // experts).astype(jnp.float32), value, 0.0)


def kernel(
    sizes,
    hid_hbm,
    gain_hbm,
    left_hbm,
    right_hbm,
    ids_hbm,
    weights_hbm,
    scales_hbm,
    gate_hbm,
    up_hbm,
    down_hbm,
    out_ref,
    hid_ref,
    gain_ref,
    left_ref,
    right_ref,
    ids_ref,
    weights_ref,
    scales_ref,
    unit_buf,
    down_buf,
    row_out,
    row_in,
    route_out,
    route_in,
    route_t,
    lines,
    part_out,
    part_in,
    units,
    mixing,
    values,
    back_out,
    back_in,
    unit_sem,
    down_sem,
    part_recv,
    row_recv,
    back_recv,
    plain_sem,
):
    n_ep, n_tp, capacity = sizes
    peers = n_ep * n_tp
    ep = lax.axis_index("ep")
    tp = lax.axis_index("tp")
    me = ep * n_tp + tp
    held, half, ff = gate_hbm.shape
    unit_ring, pair, deep, _ = unit_buf.shape
    down_ring, group, _, wide = down_buf.shape
    rows = hid_ref.shape[0]
    fold = SUBLANES // rows
    block = rows * n_tp
    slots = capacity * n_ep
    experts = held * n_ep // 2
    padded = peers * SUBLANES
    split = half // deep
    thin = deep // fold
    chunks = half // wide
    parts = held // group
    items = chunks * parts
    steps = held // pair
    pieces = split * steps
    lag = min(LAG, steps)
    slim = wide // fold

    barrier = pltpu.get_barrier_semaphore()

    def start_unit(i, slot):
        k, s = i // steps, lax.rem(i, steps)
        for source, at in ((gate_hbm, 0), (up_hbm, ff)):
            pltpu.make_async_copy(
                source.at[pl.ds(s * pair, pair), pl.ds(pl.multiple_of(k * deep, deep), deep)],
                unit_buf.at[slot, :, :, pl.ds(at, ff)],
                unit_sem.at[slot],
            ).start()

    def start_down(i, slot):
        c, q = i // parts, lax.rem(i, parts)
        pltpu.make_async_copy(
            down_hbm.at[pl.ds(q * group, group), :, pl.ds(pl.multiple_of(c * wide, wide), wide)],
            down_buf.at[slot],
            down_sem.at[slot],
        ).start()

    def start_downs():
        for i in range(down_ring):
            start_down(jnp.int32(i), i)

    def landed(ref, sem):
        pltpu.make_async_copy(ref, ref, sem).wait()

    def drain(ref, count, sem):
        landed(ref.at[pl.ds(0, count)], sem)

    def each(first, count, act):
        if count <= UNROLL:
            for offset in range(first, count):
                act(offset)
        else:
            pl.loop(first, count)(act)

    def each_peer(act):
        def visit(offset):
            peer = lax.rem(me + offset, peers)
            act({"ep": peer // n_tp, "tp": lax.rem(peer, n_tp)}, peer)

        each(1, peers, visit)

    small = [
        pltpu.make_async_copy(source, target, plain_sem.at[4])
        for source, target in (
            (hid_hbm, hid_ref),
            (gain_hbm, gain_ref),
            (left_hbm, left_ref),
            (right_hbm, right_ref),
            (ids_hbm, ids_ref),
            (weights_hbm, weights_ref),
            (scales_hbm, scales_ref),
        )
    ]
    for copy in small:
        copy.start()
    each_peer(
        lambda where, peer: pl.semaphore_signal(barrier, inc=1, device_id=where, device_id_type=MESH)
    )
    early = min(EARLY, unit_ring)
    for i in range(early):
        start_unit(jnp.int32(i), i)
    for copy in small:
        copy.wait()

    route = routing(ids_ref, weights_ref, experts, capacity)
    route_out[...] = route
    route_in[ep] = route
    rotated = rotate(hid_ref, gain_ref, left_ref, right_ref, n_tp).astype(jnp.float32)
    for k in range(split):
        for h in range(n_tp):
            line = rotated[h * rows : (h + 1) * rows, k * deep : (k + 1) * deep]
            line = jnp.concatenate([line[:, f * thin : (f + 1) * thin] for f in range(fold)], axis=0)
            row_out[k, h] = line.astype(jnp.bfloat16)
        row_in[k, me] = row_out[k, tp]

    pl.semaphore_wait(barrier, peers - 1)

    def send_route(offset):
        pltpu.make_async_remote_copy(
            src_ref=route_out,
            dst_ref=route_in.at[ep],
            send_sem=plain_sem.at[0],
            recv_sem=plain_sem.at[1],
            device_id={"ep": lax.rem(ep + offset, n_ep), "tp": tp},
            device_id_type=MESH,
        ).start()

    def send_row(k):
        def act(where, peer):
            pltpu.make_async_remote_copy(
                src_ref=row_out.at[k, lax.rem(peer, n_tp)],
                dst_ref=row_in.at[k, me],
                send_sem=plain_sem.at[2],
                recv_sem=row_recv.at[k],
                device_id=where,
                device_id_type=MESH,
            ).start()

        return act

    each(1, n_ep, send_route)
    for k in range(split):
        each_peer(send_row(k))

    for i in range(early, unit_ring):
        start_unit(jnp.int32(i), i)
    if pieces <= unit_ring:
        start_downs()

    drain(route_in, n_ep - 1, plain_sem.at[1])
    spread = []
    for b in range(n_ep):
        for h in range(n_tp):
            spread.append(route_in[b, h * rows : (h + 1) * rows, :])
            spread.append(jnp.zeros((SUBLANES - rows, capacity * experts), jnp.float32))
    route_t[...] = jnp.concatenate(spread, axis=0).T
    first = lax.rem(ep * held, experts)
    owner = (
        iota((n_ep, padded), 1) // (n_tp * SUBLANES) == iota((n_ep, padded), 0)
    ).astype(jnp.float32)
    picks = []
    for c in range(capacity):
        line = route_t[pl.ds(c * experts + first, held), :]
        picks.append((line[:, None, :] * owner[None, :, :])[:, None])
    weighted = jnp.concatenate(picks, axis=1).reshape(held * slots, padded)
    shifted = [weighted] + [pltpu.roll(weighted, f * rows, 1) for f in range(1, fold)]
    chosen = jnp.concatenate(shifted, axis=0)
    chosen = jnp.where(chosen > 0.0, 1.0, 0.0).astype(jnp.bfloat16)
    for f in range(fold):
        mixing[:, f * held * slots : (f + 1) * held * slots] = shifted[f].T.astype(jnp.bfloat16)

    def select(k):
        picked = jnp.dot(
            chosen, row_in[k].reshape(padded, thin), preferred_element_type=jnp.float32
        ).astype(jnp.bfloat16)
        for f in range(fold):
            lines[k, :, :, f * thin : (f + 1) * thin] = picked[
                f * held * slots : (f + 1) * held * slots
            ].reshape(held, slots, thin)

    def part_copy(s):
        return pltpu.make_async_remote_copy(
            src_ref=part_out.at[pl.ds(s * pair, pair)],
            dst_ref=part_in.at[pl.ds(s * pair, pair)],
            send_sem=plain_sem.at[0],
            recv_sem=part_recv.at[s],
            device_id={"ep": ep, "tp": 1 - tp},
            device_id_type=MESH,
        )

    def finish(s):
        for p in range(pair):
            j = s * pair + p
            scale = scales_ref[j]
            gate = (part_out[j, :, pl.ds(0, ff)] + part_in[j, :, pl.ds(0, ff)]) * scale[0:1]
            up = (part_out[j, :, pl.ds(ff, ff)] + part_in[j, :, pl.ds(ff, ff)]) * scale[1:2]
            units[j] = (gate / (1.0 + jnp.exp(-gate)) * up).astype(jnp.bfloat16)

    def project(k, s, slot):
        for p in range(pair):
            j = s * pair + p
            total = jnp.dot(lines[k, j], unit_buf[slot, p], preferred_element_type=jnp.float32)
            if k > 0:
                total = total + part_out[j]
            part_out[j] = total

    def step(k, s, both):
        i = k * steps + s
        slot = lax.rem(i, unit_ring)
        landed(unit_buf.at[slot], unit_sem.at[slot])
        if both:
            part_copy(s - lag).wait_recv()
            finish(s - lag)
        project(k, s, slot)
        if k == split - 1:
            part_copy(s).start()
        if pieces > unit_ring:

            @pl.when(i + unit_ring < pieces)
            def _():
                start_unit(i + unit_ring, slot)

            @pl.when(i + unit_ring == pieces - 1)
            def _():
                start_downs()

    drain(route_in, n_ep - 1, plain_sem.at[0])
    for k in range(split):
        drain(row_in.at[k], peers - 1, row_recv.at[k])
        select(k)
        if k < split - 1:

            @pl.loop(0, steps)
            def _(s):
                step(k, s, False)

    for s in range(lag):
        step(split - 1, jnp.int32(s), False)

    @pl.loop(lag, steps)
    def _(s):
        step(split - 1, s, True)

    def down_wait(c, q):
        slot = lax.rem(c * parts + q, down_ring)
        landed(down_buf.at[slot], down_sem.at[slot])

    def down_part(c, q):
        slot = lax.rem(c * parts + q, down_ring)
        for p in range(group):
            j = q * group + p
            value = jnp.dot(units[j], down_buf[slot, p], preferred_element_type=jnp.float32)
            for f in range(fold):
                at = f * held * slots + j * slots
                values[at : at + slots, :] = value[:, f * slim : (f + 1) * slim].astype(jnp.bfloat16)

    def down_next(c, q):
        i = c * parts + q

        @pl.when(i + down_ring < items)
        def _():
            start_down(i + down_ring, lax.rem(i, down_ring))

    def give(c):
        mixed = jnp.dot(mixing[...], values[...], preferred_element_type=jnp.float32)
        back_out[c] = mixed.astype(jnp.bfloat16).reshape(peers, SUBLANES, slim)
        back_in[c, me] = back_out[c, me]

        def act(where, peer):
            pltpu.make_async_remote_copy(
                src_ref=back_out.at[c, peer],
                dst_ref=back_in.at[c, me],
                send_sem=plain_sem.at[3],
                recv_sem=back_recv.at[c],
                device_id=where,
                device_id_type=MESH,
            ).start()

        each_peer(act)

    ready = (steps - lag) * pair // group
    zero = jnp.int32(0)
    for q in range(ready):
        down_wait(zero, q)
        down_part(zero, q)
        down_next(zero, q)
    for s in range(steps - lag, steps):
        part_copy(jnp.int32(s)).wait_recv()
        finish(jnp.int32(s))
    for q in range(ready, parts):
        down_wait(zero, q)
        down_part(zero, q)
        down_next(zero, q)
    give(zero)

    @pl.loop(1, chunks)
    def _(c):
        for q in range(parts):
            down_wait(c, q)
            down_part(c, q)
            down_next(c, q)
        give(c)

    for c in range(chunks):
        drain(back_in.at[c], peers - 1, back_recv.at[c])
        for h in range(n_tp):
            total = back_in[c, h].astype(jnp.float32)
            for e in range(1, n_ep):
                total = total + back_in[c, e * n_tp + h].astype(jnp.float32)
            for f in range(fold):
                at = h * half + c * wide + f * slim
                out_ref[:, at : at + slim] = total[f * rows : (f + 1) * rows].astype(jnp.bfloat16)
    landed(part_out, plain_sem.at[0])
    for k in range(split):
        drain(row_in.at[k], peers - 1, plain_sem.at[2])
    for c in range(chunks):
        drain(back_in.at[c], peers - 1, plain_sem.at[3])


def body(
    hidden,
    norm_gain,
    rot_left,
    rot_right,
    expert_ids,
    gate_weights,
    w_gate,
    w_up,
    w_down,
    unit_scales,
):
    n_ep, n_tp = lax.axis_size("ep"), lax.axis_size("tp")
    peers = n_ep * n_tp
    rows, width = hidden.shape
    group_rows, choices = expert_ids.shape
    held, half, ff = w_gate.shape
    experts = held * n_ep // 2
    capacity = 5 * group_rows * choices // (2 * experts)
    slots = capacity * n_ep
    unit_pair = PAIR if held % PAIR == 0 else 1
    steps = held // unit_pair
    unit_ring = min(UNIT_RING, SPLIT * steps)
    deep = half // SPLIT
    group = min(GROUP, held)
    wide = half // CHUNKS
    down_ring = min(DOWN_RING, held // group * CHUNKS)
    fold = SUBLANES // rows
    padded = peers * SUBLANES
    small = (
        hidden,
        norm_gain.reshape(1, width),
        rot_left,
        rot_right,
        expert_ids,
        gate_weights,
        unit_scales,
    )
    return pl.pallas_call(
        functools.partial(kernel, (n_ep, n_tp, capacity)),
        out_shape=pltpu.VMEM((rows, width), jnp.bfloat16),
        in_specs=[pl.BlockSpec(memory_space=pltpu.HBM)] * 10,
        out_specs=pl.BlockSpec(memory_space=pltpu.VMEM),
        scratch_shapes=[pltpu.VMEM(x.shape, x.dtype) for x in small]
        + [
            pltpu.VMEM((unit_ring, unit_pair, deep, 2 * ff), jnp.bfloat16),
            pltpu.VMEM((down_ring, group, ff, wide), jnp.bfloat16),
            pltpu.VMEM((SPLIT, n_tp, SUBLANES, deep // fold), jnp.bfloat16),
            pltpu.VMEM((SPLIT, peers, SUBLANES, deep // fold), jnp.bfloat16),
            pltpu.VMEM((group_rows, capacity * experts), jnp.float32),
            pltpu.VMEM((n_ep, group_rows, capacity * experts), jnp.float32),
            pltpu.VMEM((capacity * experts, padded), jnp.float32),
            pltpu.VMEM((SPLIT, held, slots, deep), jnp.bfloat16),
            pltpu.VMEM((held, slots, 2 * ff), jnp.float32),
            pltpu.VMEM((held, slots, 2 * ff), jnp.float32),
            pltpu.VMEM((held, slots, ff), jnp.bfloat16),
            pltpu.VMEM((padded, fold * held * slots), jnp.bfloat16),
            pltpu.VMEM((fold * held * slots, wide // fold), jnp.bfloat16),
            pltpu.VMEM((CHUNKS, peers, SUBLANES, wide // fold), jnp.bfloat16),
            pltpu.VMEM((CHUNKS, peers, SUBLANES, wide // fold), jnp.bfloat16),
            pltpu.SemaphoreType.DMA((unit_ring,)),
            pltpu.SemaphoreType.DMA((down_ring,)),
            pltpu.SemaphoreType.DMA((steps,)),
            pltpu.SemaphoreType.DMA((SPLIT,)),
            pltpu.SemaphoreType.DMA((CHUNKS,)),
            pltpu.SemaphoreType.DMA((5,)),
        ],
        compiler_params=pltpu.CompilerParams(
            collective_id=0, has_side_effects=True, vmem_limit_bytes=63 * 1024 * 1024
        ),
    )(*small, w_gate, w_up, w_down)


def solution(mesh):
    placed = (
        P(("groups", "ep", "tp"), None),
        P(),
        P(),
        P(),
        P(("groups", "ep"), None),
        P(("groups", "ep"), None),
        P("ep", "tp", None),
        P("ep", "tp", None),
        P("ep", None, "tp"),
        P("ep", None, None),
    )
    return jax.shard_map(
        body, mesh=mesh, in_specs=placed, out_specs=P(("groups", "ep", "tp"), None), check_vma=False
    )
```

```python
import functools

import jax
import jax.numpy as jnp
from jax import lax
from jax.experimental import pallas as pl
from jax.experimental.pallas import tpu as pltpu
from jax.sharding import PartitionSpec as P

MESH = pl.DeviceIdType.MESH
HIGH = lax.Precision.HIGHEST
LANES = 128
SUBLANES = 8
PASSES = (4, 4, 2)
LAG = 2
MORE = 2
SPAN = 5
UNIT_RING = 14
DOWN_RING = 9
EARLY = 3
WIDTHS = ((1, 8), (2, 4), (2, 4), (2, 4), (1, 4))
UNROLL = 32


def iota(shape, dim):
    return lax.broadcasted_iota(jnp.int32, shape, dim)


def halves(value):
    high = value.astype(jnp.bfloat16)
    return high, (value - high.astype(jnp.float32)).astype(jnp.bfloat16)


def rotate(hid_ref, gain_ref, left_ref, right_ref, n_tp):
    values = hid_ref[...].astype(jnp.float32)
    rows, width = values.shape
    half = width // n_tp
    order = left_ref.shape[0]
    groups = half // LANES
    per_lane = LANES // order
    block = n_tp * rows
    count = block * groups * per_lane

    def line_of(index):
        return (
            (index % block) // rows * (half // order)
            + index // block % groups * per_lane
            + index // (block * groups)
        )

    across = (((1,), (1,)), ((), ()))
    spread = (line_of(iota((count, order), 0)) == iota((count, order), 1)).astype(jnp.bfloat16)
    same_row = iota((count, count), 0) % rows == iota((count, count), 1) % rows
    wide = []
    for part in halves(left_ref[...]):
        tall = jnp.dot(spread, part, preferred_element_type=jnp.float32).astype(jnp.bfloat16)
        full = lax.dot_general(tall, spread, across, preferred_element_type=jnp.float32)
        wide.append(jnp.where(same_row, full, 0.0).astype(jnp.bfloat16))

    mean_square = jnp.mean(values * values, axis=1, keepdims=True)
    normed = values * lax.rsqrt(mean_square + 1e-06) * gain_ref[...]
    stacked = jnp.concatenate([normed[:, h * half : (h + 1) * half] for h in range(n_tp)], axis=0)
    tall = jnp.concatenate(
        [stacked[:, m * LANES : (m + 1) * LANES] for m in range(groups)], axis=0
    )
    tall = jnp.concatenate(
        [tall[:, p * order : (p + 1) * order] for p in range(per_lane)], axis=0
    )

    high, low = halves(tall)
    right_high, right_low = halves(right_ref[...])
    turned = (
        lax.dot_general(high, right_high, across, preferred_element_type=jnp.float32)
        + lax.dot_general(high, right_low, across, preferred_element_type=jnp.float32)
        + lax.dot_general(low, right_high, across, preferred_element_type=jnp.float32)
    )
    high, low = halves(turned)
    turned = (
        jnp.dot(wide[0], high, preferred_element_type=jnp.float32)
        + jnp.dot(wide[0], low, preferred_element_type=jnp.float32)
        + jnp.dot(wide[1], high, preferred_element_type=jnp.float32)
    )
    step = count // per_lane
    flat = jnp.concatenate([turned[p * step : (p + 1) * step] for p in range(per_lane)], axis=1)
    return jnp.concatenate([flat[m * block : (m + 1) * block] for m in range(groups)], axis=1)


def routing(ids_ref, weights_ref, experts, capacity):
    ids = ids_ref[...]
    weights = weights_ref[...]
    rows, choices = ids.shape
    weights = weights / jnp.sum(weights, axis=1, keepdims=True)
    weights = weights.astype(jnp.bfloat16).astype(jnp.float32)
    lane = iota((rows, capacity * experts), 1)
    expert = lane % experts
    named = jnp.zeros(lane.shape, jnp.float32)
    value = jnp.zeros(lane.shape, jnp.float32)
    for k in range(choices):
        hit = (ids[:, k : k + 1] == expert).astype(jnp.float32)
        named = named + hit
        value = value + hit * weights[:, k : k + 1]
    row = iota(lane.shape, 0)
    rank = jnp.zeros(lane.shape, jnp.float32)
    for r in range(rows):
        rank = rank + jnp.where(row > r, named[r : r + 1, :], 0.0)
    return jnp.where(rank == (lane // experts).astype(jnp.float32), value, 0.0)


def passes_of(held, half):
    plan, pieces, begin = [], [], 0
    for share in PASSES:
        deep, count = half // share, share if held % share == 0 else 1
        plan.append((begin, deep, count))
        pieces += [(begin, deep, count, s) for s in range(held // count)]
        begin += deep
    return plan, pieces


def chunks_of(held, half):
    chunks, items, begin = [], [], 0
    unit = half // sum(share for share, _ in WIDTHS)
    for share, count in WIDTHS:
        count = count if held % count == 0 else 1
        chunks.append((begin, share * unit, count))
        items += [(begin, share * unit, count, q) for q in range(held // count)]
        begin += share * unit
    return chunks, items


def kernel(
    sizes,
    hid_hbm,
    gain_hbm,
    left_hbm,
    right_hbm,
    ids_hbm,
    weights_hbm,
    scales_hbm,
    gate_hbm,
    up_hbm,
    down_hbm,
    out_ref,
    hid_ref,
    gain_ref,
    left_ref,
    right_ref,
    ids_ref,
    weights_ref,
    scales_ref,
    unit_buf,
    down_buf,
    row_out,
    row_in,
    route_out,
    route_in,
    route_t,
    lines,
    part_out,
    part_in,
    units,
    mixing,
    values,
    back_out,
    back_in,
    unit_sem,
    down_sem,
    part_recv,
    row_recv,
    back_recv,
    plain_sem,
):
    n_ep, n_tp, capacity = sizes
    peers = n_ep * n_tp
    ep = lax.axis_index("ep")
    tp = lax.axis_index("tp")
    me = ep * n_tp + tp
    held, half, ff = gate_hbm.shape
    unit_ring = unit_buf.shape[0]
    down_ring = down_buf.shape[0]
    rows = hid_ref.shape[0]
    fold = SUBLANES // rows
    block = rows * n_tp
    slots = capacity * n_ep
    experts = held * n_ep // 2
    padded = peers * SUBLANES
    chunks, items = chunks_of(held, half)
    plan, pieces = passes_of(held, half)
    pair = plan[-1][2]
    pairs = held // pair
    more = MORE if pairs % MORE == 0 else 1
    lag = min(LAG, pairs // more)
    again = len(pieces) - unit_ring

    barrier = pltpu.get_barrier_semaphore()

    def start_unit(i):
        begin, deep, count, s = pieces[i]
        slot = i % unit_ring
        for p in range(count):
            for source, at in ((gate_hbm, 0), (up_hbm, ff)):
                pltpu.make_async_copy(
                    source.at[s * count + p, pl.ds(begin, deep)],
                    unit_buf.at[slot, pl.ds(p * deep, deep), pl.ds(at, ff)],
                    unit_sem.at[slot],
                ).start()

    def start_down(i):
        begin, wide, count, q = items[i]
        slot = i % down_ring
        for p in range(count):
            pltpu.make_async_copy(
                down_hbm.at[q * count + p, :, pl.ds(begin, wide)],
                down_buf.at[slot, :, pl.ds(p * wide, wide)],
                down_sem.at[slot],
            ).start()

    ahead = -(-down_ring // min(pairs, SPAN))
    since = pairs - -(-down_ring // ahead)

    def start_downs(s):
        for i in range((s - since) * ahead, min((s - since + 1) * ahead, down_ring)):
            if i >= 0:
                start_down(i)

    def landed(ref, sem):
        pltpu.make_async_copy(ref, ref, sem).wait()

    def drain(ref, count, sem):
        landed(ref.at[pl.ds(0, count)], sem)

    def each(first, count, act):
        if count <= UNROLL:
            for offset in range(first, count):
                act(offset)
        else:
            pl.loop(first, count)(act)

    upper = ep >= n_ep // 2
    own = jnp.where(upper, ep, n_ep - 1 - ep)

    def each_ep(act):
        def visit(i):
            i = i + jnp.where(i >= own, 1, 0)
            act(jnp.where(upper, i, n_ep - 1 - i))

        each(0, n_ep - 1, visit)

    def each_peer(act):
        def visit(to):
            for h in range(n_tp):
                act({"ep": to, "tp": h}, to * n_tp + h, h)

        each_ep(visit)
        for h in range(1, n_tp):
            beside = lax.rem(tp + h, n_tp)
            act({"ep": ep, "tp": beside}, ep * n_tp + beside, beside)

    small = [
        pltpu.make_async_copy(source, target, plain_sem.at[4])
        for source, target in (
            (hid_hbm, hid_ref),
            (gain_hbm, gain_ref),
            (left_hbm, left_ref),
            (right_hbm, right_ref),
            (ids_hbm, ids_ref),
            (weights_hbm, weights_ref),
            (scales_hbm, scales_ref),
        )
    ]
    for copy in small:
        copy.start()
    each_peer(
        lambda where, peer, h: pl.semaphore_signal(
            barrier, inc=1, device_id=where, device_id_type=MESH
        )
    )
    early = min(EARLY, unit_ring)
    for i in range(early):
        start_unit(i)
    for copy in small:
        copy.wait()

    route = routing(ids_ref, weights_ref, experts, capacity)
    route_out[...] = route.astype(jnp.bfloat16)
    route_in[ep] = route_out[...]
    rotated = rotate(hid_ref, gain_ref, left_ref, right_ref, n_tp).astype(jnp.float32)
    for begin, deep, _ in plan:
        thin = deep // fold
        for h in range(n_tp):
            line = rotated[h * rows : (h + 1) * rows, begin : begin + deep]
            line = jnp.concatenate([line[:, f * thin : (f + 1) * thin] for f in range(fold)], axis=0)
            row_out[h, :, begin // fold : begin // fold + thin] = line.astype(jnp.bfloat16)
    row_in[me] = row_out[tp]

    pl.semaphore_wait(barrier, peers - 1)

    def send_route(to):
        pltpu.make_async_remote_copy(
            src_ref=route_out,
            dst_ref=route_in.at[ep],
            send_sem=plain_sem.at[0],
            recv_sem=plain_sem.at[1],
            device_id={"ep": to, "tp": tp},
            device_id_type=MESH,
        ).start()

    def part_of(k):
        return pl.ds(plan[k][0] // fold, plan[k][1] // fold)

    def send_row(k):
        def act(where, peer, h):
            pltpu.make_async_remote_copy(
                src_ref=row_out.at[h, :, part_of(k)],
                dst_ref=row_in.at[me, :, part_of(k)],
                send_sem=plain_sem.at[2],
                recv_sem=row_recv.at[k],
                device_id=where,
                device_id_type=MESH,
            ).start()

        return act

    each_ep(send_route)
    for k in range(len(plan)):
        each_peer(send_row(k))

    for i in range(early, unit_ring):
        start_unit(i)

    drain(route_in, n_ep - 1, plain_sem.at[1])
    spread = []
    for b in range(n_ep):
        for h in range(n_tp):
            spread.append(route_in[b].astype(jnp.float32)[h * rows : (h + 1) * rows, :])
            spread.append(jnp.zeros((SUBLANES - rows, capacity * experts), jnp.float32))
    route_t[...] = jnp.concatenate(spread, axis=0).T
    first = lax.rem(ep * held, experts)
    owner = (
        iota((n_ep, padded), 1) // (n_tp * SUBLANES) == iota((n_ep, padded), 0)
    ).astype(jnp.float32)
    picks = []
    for c in range(capacity):
        line = route_t[pl.ds(c * experts + first, held), :]
        picks.append((line[:, None, :] * owner[None, :, :])[:, None])
    weighted = jnp.concatenate(picks, axis=1).reshape(held * slots, padded)
    shifted = [weighted] + [pltpu.roll(weighted, f * rows, 1) for f in range(1, fold)]
    chosen = jnp.concatenate(shifted, axis=0)
    chosen = jnp.where(chosen > 0.0, 1.0, 0.0).astype(jnp.bfloat16)
    for f in range(fold):
        mixing[f] = shifted[f].T.astype(jnp.bfloat16)

    def select(k):
        begin, deep, _ = plan[k]
        thin = deep // fold
        picked = jnp.dot(
            chosen, row_in[:, :, part_of(k)].reshape(padded, thin), preferred_element_type=jnp.float32
        ).astype(jnp.bfloat16)
        for f in range(fold):
            lines[:, :, begin + f * thin : begin + (f + 1) * thin] = picked[
                f * held * slots : (f + 1) * held * slots
            ].reshape(held, slots, thin)

    def part_copy(t):
        span = pl.ds(t * more * pair, more * pair)
        return pltpu.make_async_remote_copy(
            src_ref=part_out.at[span],
            dst_ref=part_in.at[span],
            send_sem=plain_sem.at[0],
            recv_sem=part_recv.at[t],
            device_id={"ep": ep, "tp": 1 - tp},
            device_id_type=MESH,
        )

    def finish(t):
        for j in range(t * more * pair, (t + 1) * more * pair):
            scale = scales_ref[j]
            gate = (part_out[j, :, pl.ds(0, ff)] + part_in[j, :, pl.ds(0, ff)]) * scale[0:1]
            up = (part_out[j, :, pl.ds(ff, ff)] + part_in[j, :, pl.ds(ff, ff)]) * scale[1:2]
            units[j] = (gate / (1.0 + jnp.exp(-gate)) * up).astype(jnp.bfloat16)

    def project(k, s, slot):
        begin, deep, count = plan[k]
        for p in range(count):
            j = s * count + p
            total = jnp.dot(
                lines[j, :, pl.ds(begin, deep)],
                unit_buf[slot, pl.ds(p * deep, deep)],
                preferred_element_type=jnp.float32,
            )
            if k > 0:
                total = total + part_out[j]
            part_out[j] = total

    def unit_wait(k, slot):
        _, deep, count = plan[k]
        landed(unit_buf.at[slot, pl.ds(0, deep * count)], unit_sem.at[slot])

    def step(k, s, i, count):
        slots_of = [(i + m) % unit_ring for m in range(count)]
        for slot in slots_of:
            unit_wait(k, slot)
        ends = k == len(plan) - 1
        turn = s // more
        if ends and turn >= lag:
            part_copy(turn - lag).wait_recv()
            finish(turn - lag)
        for m, slot in enumerate(slots_of):
            project(k, s + m, slot)
        if ends:
            part_copy(turn).start()
        for m in range(count):
            if ends:
                start_downs(s + m)
            if i + m < again:
                start_unit(i + m + unit_ring)

    drain(route_in, n_ep - 1, plain_sem.at[0])
    done = 0
    for k in range(len(plan)):
        begin, deep, count = plan[k]
        landed(row_in.at[pl.ds(0, peers - 1), :, part_of(k)], row_recv.at[k])
        select(k)
        total = held // count
        count = more if total % more == 0 else 1
        for s in range(0, total, count):
            step(k, s, done + s, count)
        done += total

    def down(span, c, before):
        for i in span:
            _, wide, count, _ = items[i]
            slot = i % down_ring
            landed(down_buf.at[slot, :, pl.ds(0, count * wide)], down_sem.at[slot])
        for act in before:
            act()
        for i in span:
            _, wide, count, q = items[i]
            slim = wide // fold
            for p in range(count):
                j = q * count + p
                value = jnp.dot(
                    units[j],
                    down_buf[i % down_ring, :, p * wide : (p + 1) * wide],
                    preferred_element_type=jnp.float32,
                ).astype(jnp.bfloat16)
                for f in range(fold):
                    values[c % 2, f, j * slots : (j + 1) * slots, :slim] = value[
                        :, f * slim : (f + 1) * slim
                    ]
        for i in span:
            if i + down_ring < len(items):
                start_down(i + down_ring)

    def window(c):
        return pl.ds(chunks[c][0] // fold, chunks[c][1] // fold)

    def mix(c):
        slim = chunks[c][1] // fold
        mixed = jnp.dot(mixing[0], values[c % 2, 0, :, :slim], preferred_element_type=jnp.float32)
        for f in range(1, fold):
            mixed = mixed + jnp.dot(
                mixing[f], values[c % 2, f, :, :slim], preferred_element_type=jnp.float32
            )
        back_out[:, :, window(c)] = mixed.astype(jnp.bfloat16).reshape(peers, SUBLANES, slim)

    def give(c):
        def act(where, peer, h):
            pltpu.make_async_remote_copy(
                src_ref=back_out.at[peer, :, window(c)],
                dst_ref=back_in.at[me, :, window(c)],
                send_sem=plain_sem.at[3],
                recv_sem=back_recv.at[c],
                device_id=where,
                device_id_type=MESH,
            ).start()

        each_peer(act)
        back_in[me, :, window(c)] = back_out[me, :, window(c)]

    turns = pairs // more

    def last_units():
        for t in range(turns - lag, turns):
            finish(t)

    ready = (turns - lag) * more * pair // chunks[0][2]
    at = 0
    for c in range(len(chunks)):
        count = held // chunks[c][2]
        span = 2 if 0 < c < len(chunks) - 1 and count % 2 == 0 else 1
        for q in range(0, count, span):
            before = []
            if c == 0 and q == ready:
                for t in range(turns - lag, turns):
                    part_copy(t).wait_recv()
                before.append(last_units)
            if c > 0 and q == 0:
                before.append(functools.partial(mix, c - 1))
            down(range(at + q, at + q + span), c, before)
            if c > 0 and q == 0:
                give(c - 1)
        at += count
    mix(len(chunks) - 1)
    give(len(chunks) - 1)

    for c in range(len(chunks)):
        begin, wide, _ = chunks[c]
        slim = wide // fold
        landed(back_in.at[pl.ds(0, peers - 1), :, window(c)], back_recv.at[c])
        for h in range(n_tp):
            total = back_in[h, :, window(c)].astype(jnp.float32)
            for e in range(1, n_ep):
                total = total + back_in[e * n_tp + h, :, window(c)].astype(jnp.float32)
            for f in range(fold):
                at = h * half + begin + f * slim
                out_ref[:, at : at + slim] = total[f * rows : (f + 1) * rows].astype(jnp.bfloat16)
    landed(part_out, plain_sem.at[0])
    drain(row_in, peers - 1, plain_sem.at[2])
    drain(back_in, peers - 1, plain_sem.at[3])


def body(
    hidden,
    norm_gain,
    rot_left,
    rot_right,
    expert_ids,
    gate_weights,
    w_gate,
    w_up,
    w_down,
    unit_scales,
):
    n_ep, n_tp = lax.axis_size("ep"), lax.axis_size("tp")
    peers = n_ep * n_tp
    rows, width = hidden.shape
    group_rows, choices = expert_ids.shape
    held, half, ff = w_gate.shape
    experts = held * n_ep // 2
    capacity = 5 * group_rows * choices // (2 * experts)
    slots = capacity * n_ep
    plan, pieces = passes_of(held, half)
    unit_ring = min(UNIT_RING, len(pieces))
    pairs = held // plan[-1][2]
    turns = pairs // MORE if pairs % MORE == 0 else pairs
    tallest = max(deep * count for _, deep, count in plan)
    chunks, items = chunks_of(held, half)
    down_ring = min(DOWN_RING, len(items))
    broad = max(wide * count for _, wide, count in chunks)
    widest = max(wide for _, wide, _ in chunks)
    fold = SUBLANES // rows
    padded = peers * SUBLANES
    small = (
        hidden,
        norm_gain.reshape(1, width),
        rot_left,
        rot_right,
        expert_ids,
        gate_weights,
        unit_scales,
    )
    return pl.pallas_call(
        functools.partial(kernel, (n_ep, n_tp, capacity)),
        out_shape=pltpu.VMEM((rows, width), jnp.bfloat16),
        in_specs=[pl.BlockSpec(memory_space=pltpu.HBM)] * 10,
        out_specs=pl.BlockSpec(memory_space=pltpu.VMEM),
        scratch_shapes=[pltpu.VMEM(x.shape, x.dtype) for x in small]
        + [
            pltpu.VMEM((unit_ring, tallest, 2 * ff), jnp.bfloat16),
            pltpu.VMEM((down_ring, ff, broad), jnp.bfloat16),
            pltpu.VMEM((n_tp, SUBLANES, half // fold), jnp.bfloat16),
            pltpu.VMEM((peers, SUBLANES, half // fold), jnp.bfloat16),
            pltpu.VMEM((group_rows, capacity * experts), jnp.bfloat16),
            pltpu.VMEM((n_ep, group_rows, capacity * experts), jnp.bfloat16),
            pltpu.VMEM((capacity * experts, padded), jnp.float32),
            pltpu.VMEM((held, slots, half), jnp.bfloat16),
            pltpu.VMEM((held, slots, 2 * ff), jnp.float32),
            pltpu.VMEM((held, slots, 2 * ff), jnp.float32),
            pltpu.VMEM((held, slots, ff), jnp.bfloat16),
            pltpu.VMEM((fold, padded, held * slots), jnp.bfloat16),
            pltpu.VMEM((2, fold, held * slots, widest // fold), jnp.bfloat16),
            pltpu.VMEM((peers, SUBLANES, half // fold), jnp.bfloat16),
            pltpu.VMEM((peers, SUBLANES, half // fold), jnp.bfloat16),
            pltpu.SemaphoreType.DMA((unit_ring,)),
            pltpu.SemaphoreType.DMA((down_ring,)),
            pltpu.SemaphoreType.DMA((turns,)),
            pltpu.SemaphoreType.DMA((len(plan),)),
            pltpu.SemaphoreType.DMA((len(chunks),)),
            pltpu.SemaphoreType.DMA((5,)),
        ],
        compiler_params=pltpu.CompilerParams(
            collective_id=0, has_side_effects=True, vmem_limit_bytes=63 * 1024 * 1024
        ),
    )(*small, w_gate, w_up, w_down)


def solution(mesh):
    placed = (
        P(("groups", "ep", "tp"), None),
        P(),
        P(),
        P(),
        P(("groups", "ep"), None),
        P(("groups", "ep"), None),
        P("ep", "tp", None),
        P("ep", "tp", None),
        P("ep", None, "tp"),
        P("ep", None, None),
    )
    return jax.shard_map(
        body, mesh=mesh, in_specs=placed, out_specs=P(("groups", "ep", "tp"), None), check_vma=False
    )
```

```python
import functools

import jax
import jax.numpy as jnp
from jax import lax
from jax.experimental import pallas as pl
from jax.experimental.pallas import tpu as pltpu
from jax.sharding import PartitionSpec as P

MESH = pl.DeviceIdType.MESH
HIGH = lax.Precision.HIGHEST
LANES = 128
SUBLANES = 8
PASSES = (4, 4, 2)
LAG = 2
MORE = 2
SINGLE = 2
LATE = 4
SPAN = 5
UNIT_RING = 14
DOWN_RING = 9
EARLY = 3
WIDTHS = ((2, 4), (2, 4), (2, 4), (1, 8), (1, 4))
UNROLL = 32


def iota(shape, dim):
    return lax.broadcasted_iota(jnp.int32, shape, dim)


def halves(value):
    high = value.astype(jnp.bfloat16)
    return high, (value - high.astype(jnp.float32)).astype(jnp.bfloat16)


def rotate(hid_ref, gain_ref, left_ref, right_ref, n_tp):
    values = hid_ref[...].astype(jnp.float32)
    rows, width = values.shape
    half = width // n_tp
    order = left_ref.shape[0]
    groups = half // LANES
    per_lane = LANES // order
    block = n_tp * rows
    count = block * groups * per_lane

    def line_of(index):
        return (
            (index % block) // rows * (half // order)
            + index // block % groups * per_lane
            + index // (block * groups)
        )

    across = (((1,), (1,)), ((), ()))
    spread = (line_of(iota((count, order), 0)) == iota((count, order), 1)).astype(jnp.bfloat16)
    same_row = iota((count, count), 0) % rows == iota((count, count), 1) % rows
    wide = []
    for part in halves(left_ref[...]):
        tall = jnp.dot(spread, part, preferred_element_type=jnp.float32).astype(jnp.bfloat16)
        full = lax.dot_general(tall, spread, across, preferred_element_type=jnp.float32)
        wide.append(jnp.where(same_row, full, 0.0).astype(jnp.bfloat16))

    mean_square = jnp.mean(values * values, axis=1, keepdims=True)
    normed = values * lax.rsqrt(mean_square + 1e-06) * gain_ref[...]
    stacked = jnp.concatenate([normed[:, h * half : (h + 1) * half] for h in range(n_tp)], axis=0)
    tall = jnp.concatenate(
        [stacked[:, m * LANES : (m + 1) * LANES] for m in range(groups)], axis=0
    )
    tall = jnp.concatenate(
        [tall[:, p * order : (p + 1) * order] for p in range(per_lane)], axis=0
    )

    high, low = halves(tall)
    right_high, right_low = halves(right_ref[...])
    turned = (
        lax.dot_general(high, right_high, across, preferred_element_type=jnp.float32)
        + lax.dot_general(high, right_low, across, preferred_element_type=jnp.float32)
        + lax.dot_general(low, right_high, across, preferred_element_type=jnp.float32)
    )
    high, low = halves(turned)
    turned = (
        jnp.dot(wide[0], high, preferred_element_type=jnp.float32)
        + jnp.dot(wide[0], low, preferred_element_type=jnp.float32)
        + jnp.dot(wide[1], high, preferred_element_type=jnp.float32)
    )
    step = count // per_lane
    flat = jnp.concatenate([turned[p * step : (p + 1) * step] for p in range(per_lane)], axis=1)
    return jnp.concatenate([flat[m * block : (m + 1) * block] for m in range(groups)], axis=1)


def routing(ids_ref, weights_ref, experts, capacity):
    ids = ids_ref[...]
    weights = weights_ref[...]
    rows, choices = ids.shape
    weights = weights / jnp.sum(weights, axis=1, keepdims=True)
    weights = weights.astype(jnp.bfloat16).astype(jnp.float32)
    lane = iota((rows, capacity * experts), 1)
    expert = lane % experts
    named = jnp.zeros(lane.shape, jnp.float32)
    value = jnp.zeros(lane.shape, jnp.float32)
    for k in range(choices):
        hit = (ids[:, k : k + 1] == expert).astype(jnp.float32)
        named = named + hit
        value = value + hit * weights[:, k : k + 1]
    row = iota(lane.shape, 0)
    rank = jnp.zeros(lane.shape, jnp.float32)
    for r in range(rows):
        rank = rank + jnp.where(row > r, named[r : r + 1, :], 0.0)
    return jnp.where(rank == (lane // experts).astype(jnp.float32), value, 0.0)


def passes_of(held, half):
    plan, pieces, begin = [], [], 0
    for share in PASSES:
        deep, count = half // share, share if held % share == 0 else 1
        plan.append((begin, deep, count))
        pieces += [(begin, deep, count, s) for s in range(held // count)]
        begin += deep
    return plan, pieces


def blocks_of(count, step):
    return [(at, min(step, count - at)) for at in range(0, count, step)]


def spans_of(count, last):
    return blocks_of(count - 2, 2) + [(count - 2, 1), (count - 1, 1)] if last and count > 2 else blocks_of(count, 1)


def turns_of(pairs):
    single = min(SINGLE, pairs)
    return blocks_of(pairs - single, MORE) + [(s, 1) for s in range(pairs - single, pairs)]


def chunks_of(held, half):
    chunks, items, begin = [], [], 0
    unit = half // sum(share for share, _ in WIDTHS)
    for share, count in WIDTHS:
        count = count if held % count == 0 else 1
        chunks.append((begin, share * unit, count))
        items += [(begin, share * unit, count, q) for q in range(held // count)]
        begin += share * unit
    return chunks, items


def kernel(
    sizes,
    hid_hbm,
    gain_hbm,
    left_hbm,
    right_hbm,
    ids_hbm,
    weights_hbm,
    scales_hbm,
    gate_hbm,
    up_hbm,
    down_hbm,
    out_ref,
    hid_ref,
    gain_ref,
    left_ref,
    right_ref,
    ids_ref,
    weights_ref,
    scales_ref,
    unit_buf,
    down_buf,
    row_out,
    row_in,
    route_out,
    route_in,
    route_t,
    lines,
    part_out,
    part_in,
    units,
    mixing,
    values,
    back_out,
    back_in,
    unit_sem,
    part_recv,
    row_recv,
    back_recv,
    plain_sem,
):
    n_ep, n_tp, capacity = sizes
    peers = n_ep * n_tp
    ep = lax.axis_index("ep")
    tp = lax.axis_index("tp")
    me = ep * n_tp + tp
    held, half, ff = gate_hbm.shape
    unit_ring = unit_buf.shape[0]
    down_ring = down_buf.shape[0]
    rows = hid_ref.shape[0]
    fold = SUBLANES // rows
    block = rows * n_tp
    slots = capacity * n_ep
    experts = held * n_ep // 2
    padded = peers * SUBLANES
    chunks, items = chunks_of(held, half)
    plan, pieces = passes_of(held, half)
    pair = plan[-1][2]
    pairs = held // pair
    turns = turns_of(pairs)
    lag = min(LAG, len(turns))
    again = len(pieces) - unit_ring
    spare = max(again, 0)

    barrier = pltpu.get_barrier_semaphore()

    def start_unit(i):
        begin, deep, count, s = pieces[i]
        slot = i % unit_ring
        for p in range(count):
            for source, at in ((gate_hbm, 0), (up_hbm, ff)):
                pltpu.make_async_copy(
                    source.at[s * count + p, pl.ds(begin, deep)],
                    unit_buf.at[slot, pl.ds(p * deep, deep), pl.ds(at, ff)],
                    unit_sem.at[slot],
                ).start()

    def start_down(i):
        begin, wide, count, q = items[i]
        slot = i % down_ring
        for p in range(count):
            pltpu.make_async_copy(
                down_hbm.at[q * count + p, :, pl.ds(begin, wide)],
                down_buf.at[slot, :, pl.ds(p * wide, wide)],
                unit_sem.at[spare + slot],
            ).start()

    ahead = -(-down_ring // min(pairs, SPAN))
    since = pairs - -(-down_ring // ahead)

    def start_downs(s):
        for i in range((s - since) * ahead, min((s - since + 1) * ahead, down_ring)):
            if i >= 0:
                start_down(i)

    def landed(ref, sem):
        pltpu.make_async_copy(ref, ref, sem).wait()

    def drain(ref, count, sem):
        landed(ref.at[pl.ds(0, count)], sem)

    def each(first, count, act):
        if count <= UNROLL:
            for offset in range(first, count):
                act(offset)
        else:
            pl.loop(first, count)(act)

    upper = ep >= n_ep // 2
    own = jnp.where(upper, ep, n_ep - 1 - ep)

    def each_ep(act):
        def visit(i):
            i = i + jnp.where(i >= own, 1, 0)
            act(jnp.where(upper, i, n_ep - 1 - i))

        each(0, n_ep - 1, visit)

    def each_peer(act):
        def visit(to):
            for h in range(n_tp):
                act({"ep": to, "tp": h}, to * n_tp + h, h)

        each_ep(visit)
        for h in range(1, n_tp):
            beside = lax.rem(tp + h, n_tp)
            act({"ep": ep, "tp": beside}, ep * n_tp + beside, beside)

    small = [
        pltpu.make_async_copy(source, target, plain_sem.at[4])
        for source, target in (
            (hid_hbm, hid_ref),
            (gain_hbm, gain_ref),
            (left_hbm, left_ref),
            (right_hbm, right_ref),
            (ids_hbm, ids_ref),
            (weights_hbm, weights_ref),
            (scales_hbm, scales_ref),
        )
    ]
    for copy in small:
        copy.start()
    each_peer(
        lambda where, peer, h: pl.semaphore_signal(
            barrier, inc=1, device_id=where, device_id_type=MESH
        )
    )
    early = min(EARLY, unit_ring)
    for i in range(early):
        start_unit(i)
    for copy in small:
        copy.wait()

    route = routing(ids_ref, weights_ref, experts, capacity)
    route_out[...] = route.astype(jnp.bfloat16)
    route_in[ep] = route_out[...]
    rotated = rotate(hid_ref, gain_ref, left_ref, right_ref, n_tp).astype(jnp.float32)
    for begin, deep, _ in plan:
        thin = deep // fold
        for h in range(n_tp):
            line = rotated[h * rows : (h + 1) * rows, begin : begin + deep]
            line = jnp.concatenate([line[:, f * thin : (f + 1) * thin] for f in range(fold)], axis=0)
            row_out[h, :, begin // fold : begin // fold + thin] = line.astype(jnp.bfloat16)
    row_in[me] = row_out[tp]

    pl.semaphore_wait(barrier, peers - 1)

    def send_route(to):
        pltpu.make_async_remote_copy(
            src_ref=route_out,
            dst_ref=route_in.at[ep],
            send_sem=plain_sem.at[0],
            recv_sem=plain_sem.at[1],
            device_id={"ep": to, "tp": tp},
            device_id_type=MESH,
        ).start()

    def part_of(k):
        return pl.ds(plan[k][0] // fold, plan[k][1] // fold)

    def send_row(k):
        def act(where, peer, h):
            pltpu.make_async_remote_copy(
                src_ref=row_out.at[h, :, part_of(k)],
                dst_ref=row_in.at[me, :, part_of(k)],
                send_sem=plain_sem.at[2],
                recv_sem=row_recv.at[k],
                device_id=where,
                device_id_type=MESH,
            ).start()

        return act

    each_ep(send_route)
    for k in range(len(plan)):
        each_peer(send_row(k))

    for i in range(early, unit_ring):
        start_unit(i)

    drain(route_in, n_ep - 1, plain_sem.at[1])
    spread = []
    for b in range(n_ep):
        for h in range(n_tp):
            spread.append(route_in[b].astype(jnp.float32)[h * rows : (h + 1) * rows, :])
            spread.append(jnp.zeros((SUBLANES - rows, capacity * experts), jnp.float32))
    route_t[...] = jnp.concatenate(spread, axis=0).T
    first = lax.rem(ep * held, experts)
    owner = (
        iota((n_ep, padded), 1) // (n_tp * SUBLANES) == iota((n_ep, padded), 0)
    ).astype(jnp.float32)
    picks = []
    for c in range(capacity):
        line = route_t[pl.ds(c * experts + first, held), :]
        picks.append((line[:, None, :] * owner[None, :, :])[:, None])
    weighted = jnp.concatenate(picks, axis=1).reshape(held * slots, padded)
    shifted = [weighted] + [pltpu.roll(weighted, f * rows, 1) for f in range(1, fold)]
    chosen = jnp.concatenate(shifted, axis=0)
    chosen = jnp.where(chosen > 0.0, 1.0, 0.0).astype(jnp.bfloat16)
    for f in range(fold):
        mixing[f] = shifted[f].T.astype(jnp.bfloat16)

    def select(k):
        begin, deep, _ = plan[k]
        thin = deep // fold
        picked = jnp.dot(
            chosen, row_in[:, :, part_of(k)].reshape(padded, thin), preferred_element_type=jnp.float32
        ).astype(jnp.bfloat16)
        for f in range(fold):
            lines[:, :, begin + f * thin : begin + (f + 1) * thin] = picked[
                f * held * slots : (f + 1) * held * slots
            ].reshape(held, slots, thin)

    def part_copy(t):
        span = pl.ds(turns[t][0] * pair, turns[t][1] * pair)
        return pltpu.make_async_remote_copy(
            src_ref=part_out.at[span],
            dst_ref=part_in.at[span],
            send_sem=plain_sem.at[0],
            recv_sem=part_recv.at[t],
            device_id={"ep": ep, "tp": 1 - tp},
            device_id_type=MESH,
        )

    def finish(t):
        for j in range(turns[t][0] * pair, (turns[t][0] + turns[t][1]) * pair):
            scale = scales_ref[j]
            gate = (part_out[j, :, pl.ds(0, ff)] + part_in[j, :, pl.ds(0, ff)]) * scale[0:1]
            up = (part_out[j, :, pl.ds(ff, ff)] + part_in[j, :, pl.ds(ff, ff)]) * scale[1:2]
            units[j] = (gate / (1.0 + jnp.exp(-gate)) * up).astype(jnp.bfloat16)

    def project(k, s, slot):
        begin, deep, count = plan[k]
        for p in range(count):
            j = s * count + p
            total = jnp.dot(
                lines[j, :, pl.ds(begin, deep)],
                unit_buf[slot, pl.ds(p * deep, deep)],
                preferred_element_type=jnp.float32,
            )
            if k > 0:
                total = total + part_out[j]
            part_out[j] = total

    def unit_wait(k, slot):
        _, deep, count = plan[k]
        landed(unit_buf.at[slot, pl.ds(0, deep * count)], unit_sem.at[slot])

    def step(k, s, i, count, turn):
        slots_of = [(i + m) % unit_ring for m in range(count)]
        for slot in slots_of:
            unit_wait(k, slot)
        if turn is not None and turn >= lag:
            part_copy(turn - lag).wait_recv()
            finish(turn - lag)
        for m, slot in enumerate(slots_of):
            project(k, s + m, slot)
        for m in range(count):
            if i + m < again:
                start_unit(i + m + unit_ring)
        if turn is not None:
            part_copy(turn).start()
            for m in range(count):
                start_downs(s + m)

    drain(route_in, n_ep - 1, plain_sem.at[0])
    done = 0
    for k in range(len(plan)):
        begin, deep, count = plan[k]
        landed(row_in.at[pl.ds(0, peers - 1), :, part_of(k)], row_recv.at[k])
        select(k)
        total = held // count
        if k == len(plan) - 1:
            for t, (at, span) in enumerate(turns):
                step(k, at, done + at, span, t)
        else:
            for at, span in blocks_of(total, MORE):
                step(k, at, done + at, span, None)
        done += total

    def down(span, c, before):
        for i in span:
            _, wide, count, _ = items[i]
            slot = i % down_ring
            landed(down_buf.at[slot, :, pl.ds(0, count * wide)], unit_sem.at[spare + slot])
        for act in before:
            act()
        for i in span:
            _, wide, count, q = items[i]
            slim = wide // fold
            for p in range(count):
                j = q * count + p
                value = jnp.dot(
                    units[j],
                    down_buf[i % down_ring, :, p * wide : (p + 1) * wide],
                    preferred_element_type=jnp.float32,
                ).astype(jnp.bfloat16)
                for f in range(fold):
                    values[c % 2, f, j * slots : (j + 1) * slots, :slim] = value[
                        :, f * slim : (f + 1) * slim
                    ]
        for i in span:
            if i + down_ring < len(items):
                start_down(i + down_ring)

    def window(c):
        return pl.ds(chunks[c][0] // fold, chunks[c][1] // fold)

    def mix(c):
        slim = chunks[c][1] // fold
        mixed = jnp.dot(mixing[0], values[c % 2, 0, :, :slim], preferred_element_type=jnp.float32)
        for f in range(1, fold):
            mixed = mixed + jnp.dot(
                mixing[f], values[c % 2, f, :, :slim], preferred_element_type=jnp.float32
            )
        back_out[:, :, window(c)] = mixed.astype(jnp.bfloat16).reshape(peers, SUBLANES, slim)

    def give(c):
        def act(where, peer, h):
            pltpu.make_async_remote_copy(
                src_ref=back_out.at[peer, :, window(c)],
                dst_ref=back_in.at[me, :, window(c)],
                send_sem=plain_sem.at[3],
                recv_sem=back_recv.at[c],
                device_id=where,
                device_id_type=MESH,
            ).start()

        each_peer(act)
        back_in[me, :, window(c)] = back_out[me, :, window(c)]

    finished = len(turns) - lag

    def meet(experts):
        nonlocal finished
        acts = []
        while finished < len(turns) and turns[finished][0] * pair < experts:
            part_copy(finished).wait_recv()
            acts.append(functools.partial(finish, finished))
            finished += 1
        return acts

    at = 0
    for c in range(len(chunks)):
        _, _, each_item = chunks[c]
        count = held // each_item
        late = c >= len(chunks) - LATE
        for q, span in spans_of(count, c == len(chunks) - 1):
            before = meet((q + span) * each_item)
            if late and q == 0:
                before.append(functools.partial(mix, c - 1))
            down(range(at + q, at + q + span), c, before)
            if late and q == 0:
                give(c - 1)
        if c < len(chunks) - 1 - LATE:
            mix(c)
            give(c)
        at += count
    mix(len(chunks) - 1)
    give(len(chunks) - 1)

    for c in range(len(chunks)):
        begin, wide, _ = chunks[c]
        slim = wide // fold
        landed(back_in.at[pl.ds(0, peers - 1), :, window(c)], back_recv.at[c])
        for h in range(n_tp):
            total = back_in[h, :, window(c)].astype(jnp.float32)
            for e in range(1, n_ep):
                total = total + back_in[e * n_tp + h, :, window(c)].astype(jnp.float32)
            for f in range(fold):
                at = h * half + begin + f * slim
                out_ref[:, at : at + slim] = total[f * rows : (f + 1) * rows].astype(jnp.bfloat16)
    landed(part_out, plain_sem.at[0])
    drain(row_in, peers - 1, plain_sem.at[2])
    drain(back_in, peers - 1, plain_sem.at[3])


def body(
    hidden,
    norm_gain,
    rot_left,
    rot_right,
    expert_ids,
    gate_weights,
    w_gate,
    w_up,
    w_down,
    unit_scales,
):
    n_ep, n_tp = lax.axis_size("ep"), lax.axis_size("tp")
    peers = n_ep * n_tp
    rows, width = hidden.shape
    group_rows, choices = expert_ids.shape
    held, half, ff = w_gate.shape
    experts = held * n_ep // 2
    capacity = 5 * group_rows * choices // (2 * experts)
    slots = capacity * n_ep
    plan, pieces = passes_of(held, half)
    unit_ring = min(UNIT_RING, len(pieces))
    pairs = held // plan[-1][2]
    turns = len(turns_of(pairs))
    tallest = max(deep * count for _, deep, count in plan)
    chunks, items = chunks_of(held, half)
    down_ring = min(DOWN_RING, len(items))
    broad = max(wide * count for _, wide, count in chunks)
    widest = max(wide for _, wide, _ in chunks)
    fold = SUBLANES // rows
    padded = peers * SUBLANES
    small = (
        hidden,
        norm_gain.reshape(1, width),
        rot_left,
        rot_right,
        expert_ids,
        gate_weights,
        unit_scales,
    )
    return pl.pallas_call(
        functools.partial(kernel, (n_ep, n_tp, capacity)),
        out_shape=pltpu.VMEM((rows, width), jnp.bfloat16),
        in_specs=[pl.BlockSpec(memory_space=pltpu.HBM)] * 10,
        out_specs=pl.BlockSpec(memory_space=pltpu.VMEM),
        scratch_shapes=[pltpu.VMEM(x.shape, x.dtype) for x in small]
        + [
            pltpu.VMEM((unit_ring, tallest, 2 * ff), jnp.bfloat16),
            pltpu.VMEM((down_ring, ff, broad), jnp.bfloat16),
            pltpu.VMEM((n_tp, SUBLANES, half // fold), jnp.bfloat16),
            pltpu.VMEM((peers, SUBLANES, half // fold), jnp.bfloat16),
            pltpu.VMEM((group_rows, capacity * experts), jnp.bfloat16),
            pltpu.VMEM((n_ep, group_rows, capacity * experts), jnp.bfloat16),
            pltpu.VMEM((capacity * experts, padded), jnp.float32),
            pltpu.VMEM((held, slots, half), jnp.bfloat16),
            pltpu.VMEM((held, slots, 2 * ff), jnp.float32),
            pltpu.VMEM((held, slots, 2 * ff), jnp.float32),
            pltpu.VMEM((held, slots, ff), jnp.bfloat16),
            pltpu.VMEM((fold, padded, held * slots), jnp.bfloat16),
            pltpu.VMEM((2, fold, held * slots, widest // fold), jnp.bfloat16),
            pltpu.VMEM((peers, SUBLANES, half // fold), jnp.bfloat16),
            pltpu.VMEM((peers, SUBLANES, half // fold), jnp.bfloat16),
            pltpu.SemaphoreType.DMA((max(unit_ring, len(pieces) - unit_ring + down_ring),)),
            pltpu.SemaphoreType.DMA((turns,)),
            pltpu.SemaphoreType.DMA((len(plan),)),
            pltpu.SemaphoreType.DMA((len(chunks),)),
            pltpu.SemaphoreType.DMA((5,)),
        ],
        compiler_params=pltpu.CompilerParams(
            collective_id=0, has_side_effects=True, vmem_limit_bytes=63 * 1024 * 1024
        ),
    )(*small, w_gate, w_up, w_down)


def solution(mesh):
    placed = (
        P(("groups", "ep", "tp"), None),
        P(),
        P(),
        P(),
        P(("groups", "ep"), None),
        P(("groups", "ep"), None),
        P("ep", "tp", None),
        P("ep", "tp", None),
        P("ep", None, "tp"),
        P("ep", None, None),
    )
    return jax.shard_map(
        body, mesh=mesh, in_specs=placed, out_specs=P(("groups", "ep", "tp"), None), check_vma=False
    )
```

```python
import functools

import jax
import jax.numpy as jnp
from jax import lax
from jax.experimental import pallas as pl
from jax.experimental.pallas import tpu as pltpu
from jax.sharding import PartitionSpec as P

MESH = pl.DeviceIdType.MESH
HIGH = lax.Precision.HIGHEST
LANES = 128
SUBLANES = 8
PASSES = (4, 4, 2)
LAG = 2
MORE = 2
SINGLE = 2
LATE = 4
SPAN = 5
UNIT_RING = 14
DOWN_RING = 9
EARLY = 3
WIDTHS = ((2, 4), (2, 4), (2, 4), (1, 8), (1, 8))
UNROLL = 32


def iota(shape, dim):
    return lax.broadcasted_iota(jnp.int32, shape, dim)


def halves(value):
    high = value.astype(jnp.bfloat16)
    return high, (value - high.astype(jnp.float32)).astype(jnp.bfloat16)


def rotate(hid_ref, gain_ref, left_ref, right_ref, n_tp):
    values = hid_ref[...].astype(jnp.float32)
    rows, width = values.shape
    half = width // n_tp
    order = left_ref.shape[0]
    groups = half // LANES
    per_lane = LANES // order
    block = n_tp * rows
    count = block * groups * per_lane

    def line_of(index):
        return (
            (index % block) // rows * (half // order)
            + index // block % groups * per_lane
            + index // (block * groups)
        )

    across = (((1,), (1,)), ((), ()))
    spread = (line_of(iota((count, order), 0)) == iota((count, order), 1)).astype(jnp.bfloat16)
    same_row = iota((count, count), 0) % rows == iota((count, count), 1) % rows
    wide = []
    for part in halves(left_ref[...]):
        tall = jnp.dot(spread, part, preferred_element_type=jnp.float32).astype(jnp.bfloat16)
        full = lax.dot_general(tall, spread, across, preferred_element_type=jnp.float32)
        wide.append(jnp.where(same_row, full, 0.0).astype(jnp.bfloat16))

    mean_square = jnp.mean(values * values, axis=1, keepdims=True)
    normed = values * lax.rsqrt(mean_square + 1e-06) * gain_ref[...]
    stacked = jnp.concatenate([normed[:, h * half : (h + 1) * half] for h in range(n_tp)], axis=0)
    tall = jnp.concatenate(
        [stacked[:, m * LANES : (m + 1) * LANES] for m in range(groups)], axis=0
    )
    tall = jnp.concatenate(
        [tall[:, p * order : (p + 1) * order] for p in range(per_lane)], axis=0
    )

    high, low = halves(tall)
    right_high, right_low = halves(right_ref[...])
    turned = (
        lax.dot_general(high, right_high, across, preferred_element_type=jnp.float32)
        + lax.dot_general(high, right_low, across, preferred_element_type=jnp.float32)
        + lax.dot_general(low, right_high, across, preferred_element_type=jnp.float32)
    )
    high, low = halves(turned)
    turned = (
        jnp.dot(wide[0], high, preferred_element_type=jnp.float32)
        + jnp.dot(wide[0], low, preferred_element_type=jnp.float32)
        + jnp.dot(wide[1], high, preferred_element_type=jnp.float32)
    )
    step = count // per_lane
    flat = jnp.concatenate([turned[p * step : (p + 1) * step] for p in range(per_lane)], axis=1)
    return jnp.concatenate([flat[m * block : (m + 1) * block] for m in range(groups)], axis=1)


def routing(ids_ref, weights_ref, experts, capacity):
    ids = ids_ref[...]
    weights = weights_ref[...]
    rows, choices = ids.shape
    weights = weights / jnp.sum(weights, axis=1, keepdims=True)
    weights = weights.astype(jnp.bfloat16).astype(jnp.float32)
    lane = iota((rows, capacity * experts), 1)
    expert = lane % experts
    named = jnp.zeros(lane.shape, jnp.float32)
    value = jnp.zeros(lane.shape, jnp.float32)
    for k in range(choices):
        hit = (ids[:, k : k + 1] == expert).astype(jnp.float32)
        named = named + hit
        value = value + hit * weights[:, k : k + 1]
    row = iota(lane.shape, 0)
    rank = jnp.zeros(lane.shape, jnp.float32)
    for r in range(rows):
        rank = rank + jnp.where(row > r, named[r : r + 1, :], 0.0)
    return jnp.where(rank == (lane // experts).astype(jnp.float32), value, 0.0)


def passes_of(held, half):
    plan, pieces, begin = [], [], 0
    for share in PASSES:
        deep, count = half // share, share if held % share == 0 else 1
        plan.append((begin, deep, count))
        pieces += [(begin, deep, count, s) for s in range(held // count)]
        begin += deep
    return plan, pieces


def blocks_of(count, step):
    return [(at, min(step, count - at)) for at in range(0, count, step)]


def spans_of(count, last):
    return blocks_of(count - 2, 2) + [(count - 2, 1), (count - 1, 1)] if last and count > 2 else blocks_of(count, 1)


def turns_of(pairs):
    single = min(SINGLE, pairs)
    return blocks_of(pairs - single, MORE) + [(s, 1) for s in range(pairs - single, pairs)]


def chunks_of(held, half):
    chunks, items, begin = [], [], 0
    unit = half // sum(share for share, _ in WIDTHS)
    for share, count in WIDTHS:
        count = count if held % count == 0 else 1
        chunks.append((begin, share * unit, count))
        items += [(begin, share * unit, count, q) for q in range(held // count)]
        begin += share * unit
    return chunks, items


def kernel(
    sizes,
    hid_hbm,
    gain_hbm,
    left_hbm,
    right_hbm,
    ids_hbm,
    weights_hbm,
    scales_hbm,
    gate_hbm,
    up_hbm,
    down_hbm,
    out_ref,
    hid_ref,
    gain_ref,
    left_ref,
    right_ref,
    ids_ref,
    weights_ref,
    scales_ref,
    unit_buf,
    down_buf,
    row_out,
    row_in,
    route_out,
    route_in,
    route_t,
    lines,
    part_out,
    part_in,
    units,
    mixing,
    values,
    back_out,
    back_in,
    unit_sem,
    part_recv,
    row_recv,
    back_recv,
    plain_sem,
):
    n_ep, n_tp, capacity = sizes
    peers = n_ep * n_tp
    ep = lax.axis_index("ep")
    tp = lax.axis_index("tp")
    me = ep * n_tp + tp
    held, half, ff = gate_hbm.shape
    unit_ring = unit_buf.shape[0]
    down_ring = down_buf.shape[0]
    rows = hid_ref.shape[0]
    fold = SUBLANES // rows
    block = rows * n_tp
    slots = capacity * n_ep
    experts = held * n_ep // 2
    padded = peers * SUBLANES
    chunks, items = chunks_of(held, half)
    plan, pieces = passes_of(held, half)
    pair = plan[-1][2]
    pairs = held // pair
    turns = turns_of(pairs)
    lag = min(LAG, len(turns))
    again = len(pieces) - unit_ring
    spare = max(again, 0)

    barrier = pltpu.get_barrier_semaphore()

    def start_unit(i):
        begin, deep, count, s = pieces[i]
        slot = i % unit_ring
        for p in range(count):
            for source, at in ((gate_hbm, 0), (up_hbm, ff)):
                pltpu.make_async_copy(
                    source.at[s * count + p, pl.ds(begin, deep)],
                    unit_buf.at[slot, pl.ds(p * deep, deep), pl.ds(at, ff)],
                    unit_sem.at[slot],
                ).start()

    def start_down(i):
        begin, wide, count, q = items[i]
        slot = i % down_ring
        for p in range(count):
            pltpu.make_async_copy(
                down_hbm.at[q * count + p, :, pl.ds(begin, wide)],
                down_buf.at[slot, :, pl.ds(p * wide, wide)],
                unit_sem.at[spare + slot],
            ).start()

    ahead = -(-down_ring // min(pairs, SPAN))
    since = pairs - -(-down_ring // ahead)

    def start_downs(s):
        for i in range((s - since) * ahead, min((s - since + 1) * ahead, down_ring)):
            if i >= 0:
                start_down(i)

    def landed(ref, sem):
        pltpu.make_async_copy(ref, ref, sem).wait()

    def drain(ref, count, sem):
        landed(ref.at[pl.ds(0, count)], sem)

    def each(first, count, act):
        if count <= UNROLL:
            for offset in range(first, count):
                act(offset)
        else:
            pl.loop(first, count)(act)

    upper = ep >= n_ep // 2
    own = jnp.where(upper, ep, n_ep - 1 - ep)

    def each_ep(act):
        def visit(i):
            i = i + jnp.where(i >= own, 1, 0)
            act(jnp.where(upper, i, n_ep - 1 - i))

        each(0, n_ep - 1, visit)

    def each_peer(act):
        def visit(to):
            for h in range(n_tp):
                act({"ep": to, "tp": h}, to * n_tp + h, h)

        each_ep(visit)
        for h in range(1, n_tp):
            beside = lax.rem(tp + h, n_tp)
            act({"ep": ep, "tp": beside}, ep * n_tp + beside, beside)

    small = [
        pltpu.make_async_copy(source, target, plain_sem.at[4])
        for source, target in (
            (hid_hbm, hid_ref),
            (gain_hbm, gain_ref),
            (left_hbm, left_ref),
            (right_hbm, right_ref),
            (ids_hbm, ids_ref),
            (weights_hbm, weights_ref),
        )
    ]
    scales_copy = pltpu.make_async_copy(scales_hbm, scales_ref, plain_sem.at[5])
    for copy in small:
        copy.start()
    start_unit(0)
    each_peer(
        lambda where, peer, h: pl.semaphore_signal(
            barrier, inc=1, device_id=where, device_id_type=MESH
        )
    )
    early = min(EARLY, unit_ring)
    for i in range(1, early):
        start_unit(i)
    scales_copy.start()
    for copy in small:
        copy.wait()

    route = routing(ids_ref, weights_ref, experts, capacity)
    route_out[...] = route.astype(jnp.bfloat16)
    route_in[ep] = route_out[...]
    rotated = rotate(hid_ref, gain_ref, left_ref, right_ref, n_tp).astype(jnp.float32)
    for begin, deep, _ in plan:
        thin = deep // fold
        for h in range(n_tp):
            line = rotated[h * rows : (h + 1) * rows, begin : begin + deep]
            line = jnp.concatenate([line[:, f * thin : (f + 1) * thin] for f in range(fold)], axis=0)
            row_out[h, :, begin // fold : begin // fold + thin] = line.astype(jnp.bfloat16)
    row_in[me] = row_out[tp]

    pl.semaphore_wait(barrier, peers - 1)

    def send_route(to):
        pltpu.make_async_remote_copy(
            src_ref=route_out,
            dst_ref=route_in.at[ep],
            send_sem=plain_sem.at[0],
            recv_sem=plain_sem.at[1],
            device_id={"ep": to, "tp": tp},
            device_id_type=MESH,
        ).start()

    def part_of(k):
        return pl.ds(plan[k][0] // fold, plan[k][1] // fold)

    def send_row(k):
        def act(where, peer, h):
            pltpu.make_async_remote_copy(
                src_ref=row_out.at[h, :, part_of(k)],
                dst_ref=row_in.at[me, :, part_of(k)],
                send_sem=plain_sem.at[2],
                recv_sem=row_recv.at[k],
                device_id=where,
                device_id_type=MESH,
            ).start()

        return act

    each_ep(send_route)
    for k in range(len(plan)):
        each_peer(send_row(k))

    for i in range(early, unit_ring):
        start_unit(i)

    drain(route_in, n_ep - 1, plain_sem.at[1])
    spread = []
    for b in range(n_ep):
        for h in range(n_tp):
            spread.append(route_in[b].astype(jnp.float32)[h * rows : (h + 1) * rows, :])
            spread.append(jnp.zeros((SUBLANES - rows, capacity * experts), jnp.float32))
    route_t[...] = jnp.concatenate(spread, axis=0).T
    first = lax.rem(ep * held, experts)
    owner = (
        iota((n_ep, padded), 1) // (n_tp * SUBLANES) == iota((n_ep, padded), 0)
    ).astype(jnp.float32)
    picks = []
    for c in range(capacity):
        line = route_t[pl.ds(c * experts + first, held), :]
        picks.append((line[:, None, :] * owner[None, :, :])[:, None])
    weighted = jnp.concatenate(picks, axis=1).reshape(held * slots, padded)
    shifted = [weighted] + [pltpu.roll(weighted, f * rows, 1) for f in range(1, fold)]
    chosen = jnp.concatenate(shifted, axis=0)
    chosen = jnp.where(chosen > 0.0, 1.0, 0.0).astype(jnp.bfloat16)
    for f in range(fold):
        mixing[f] = shifted[f].T.astype(jnp.bfloat16)

    def select(k):
        begin, deep, _ = plan[k]
        thin = deep // fold
        picked = jnp.dot(
            chosen, row_in[:, :, part_of(k)].reshape(padded, thin), preferred_element_type=jnp.float32
        ).astype(jnp.bfloat16)
        for f in range(fold):
            lines[:, :, begin + f * thin : begin + (f + 1) * thin] = picked[
                f * held * slots : (f + 1) * held * slots
            ].reshape(held, slots, thin)

    def part_copy(t):
        span = pl.ds(turns[t][0] * pair, turns[t][1] * pair)
        return pltpu.make_async_remote_copy(
            src_ref=part_out.at[span],
            dst_ref=part_in.at[span],
            send_sem=plain_sem.at[0],
            recv_sem=part_recv.at[t],
            device_id={"ep": ep, "tp": 1 - tp},
            device_id_type=MESH,
        )

    def finish(t):
        for j in range(turns[t][0] * pair, (turns[t][0] + turns[t][1]) * pair):
            scale = scales_ref[j]
            gate = (part_out[j, :, pl.ds(0, ff)] + part_in[j, :, pl.ds(0, ff)]) * scale[0:1]
            up = (part_out[j, :, pl.ds(ff, ff)] + part_in[j, :, pl.ds(ff, ff)]) * scale[1:2]
            units[j] = (gate / (1.0 + jnp.exp(-gate)) * up).astype(jnp.bfloat16)

    def project(k, s, slot):
        begin, deep, count = plan[k]
        for p in range(count):
            j = s * count + p
            total = jnp.dot(
                lines[j, :, pl.ds(begin, deep)],
                unit_buf[slot, pl.ds(p * deep, deep)],
                preferred_element_type=jnp.float32,
            )
            if k > 0:
                total = total + part_out[j]
            part_out[j] = total

    def unit_wait(k, slot):
        _, deep, count = plan[k]
        landed(unit_buf.at[slot, pl.ds(0, deep * count)], unit_sem.at[slot])

    def step(k, s, i, count, turn):
        slots_of = [(i + m) % unit_ring for m in range(count)]
        for slot in slots_of:
            unit_wait(k, slot)
        if turn is not None and turn >= lag:
            part_copy(turn - lag).wait_recv()
            finish(turn - lag)
        for m, slot in enumerate(slots_of):
            project(k, s + m, slot)
        for m in range(count):
            if i + m < again:
                start_unit(i + m + unit_ring)
        if turn is not None:
            part_copy(turn).start()
            for m in range(count):
                start_downs(s + m)

    drain(route_in, n_ep - 1, plain_sem.at[0])
    scales_copy.wait()
    done = 0
    for k in range(len(plan)):
        begin, deep, count = plan[k]
        landed(row_in.at[pl.ds(0, peers - 1), :, part_of(k)], row_recv.at[k])
        select(k)
        total = held // count
        if k == len(plan) - 1:
            for t, (at, span) in enumerate(turns):
                step(k, at, done + at, span, t)
        else:
            for at, span in blocks_of(total, MORE):
                step(k, at, done + at, span, None)
        done += total

    def down(span, c, before):
        for i in span:
            _, wide, count, _ = items[i]
            slot = i % down_ring
            landed(down_buf.at[slot, :, pl.ds(0, count * wide)], unit_sem.at[spare + slot])
        for act in before:
            act()
        for i in span:
            _, wide, count, q = items[i]
            slim = wide // fold
            for p in range(count):
                j = q * count + p
                value = jnp.dot(
                    units[j],
                    down_buf[i % down_ring, :, p * wide : (p + 1) * wide],
                    preferred_element_type=jnp.float32,
                ).astype(jnp.bfloat16)
                for f in range(fold):
                    values[c % 2, f, j * slots : (j + 1) * slots, :slim] = value[
                        :, f * slim : (f + 1) * slim
                    ]
        for i in span:
            if i + down_ring < len(items):
                start_down(i + down_ring)

    def window(c):
        return pl.ds(chunks[c][0] // fold, chunks[c][1] // fold)

    def mix(c):
        slim = chunks[c][1] // fold
        mixed = jnp.dot(mixing[0], values[c % 2, 0, :, :slim], preferred_element_type=jnp.float32)
        for f in range(1, fold):
            mixed = mixed + jnp.dot(
                mixing[f], values[c % 2, f, :, :slim], preferred_element_type=jnp.float32
            )
        back_out[:, :, window(c)] = mixed.astype(jnp.bfloat16).reshape(peers, SUBLANES, slim)

    def give(c):
        def act(where, peer, h):
            pltpu.make_async_remote_copy(
                src_ref=back_out.at[peer, :, window(c)],
                dst_ref=back_in.at[me, :, window(c)],
                send_sem=plain_sem.at[3],
                recv_sem=back_recv.at[c],
                device_id=where,
                device_id_type=MESH,
            ).start()

        each_peer(act)
        back_in[me, :, window(c)] = back_out[me, :, window(c)]

    finished = len(turns) - lag

    def meet(experts):
        nonlocal finished
        acts = []
        while finished < len(turns) and turns[finished][0] * pair < experts:
            part_copy(finished).wait_recv()
            acts.append(functools.partial(finish, finished))
            finished += 1
        return acts

    at = 0
    for c in range(len(chunks)):
        _, _, each_item = chunks[c]
        count = held // each_item
        late = c >= len(chunks) - LATE
        for q, span in spans_of(count, c == len(chunks) - 1):
            before = meet((q + span) * each_item)
            if late and q == 0:
                before.append(functools.partial(mix, c - 1))
            down(range(at + q, at + q + span), c, before)
            if late and q == 0:
                give(c - 1)
        if c < len(chunks) - 1 - LATE:
            mix(c)
            give(c)
        at += count
    mix(len(chunks) - 1)
    give(len(chunks) - 1)

    for c in range(len(chunks)):
        begin, wide, _ = chunks[c]
        slim = wide // fold
        landed(back_in.at[pl.ds(0, peers - 1), :, window(c)], back_recv.at[c])
        for h in range(n_tp):
            total = back_in[h, :, window(c)].astype(jnp.float32)
            for e in range(1, n_ep):
                total = total + back_in[e * n_tp + h, :, window(c)].astype(jnp.float32)
            for f in range(fold):
                at = h * half + begin + f * slim
                out_ref[:, at : at + slim] = total[f * rows : (f + 1) * rows].astype(jnp.bfloat16)
    landed(part_out, plain_sem.at[0])
    drain(row_in, peers - 1, plain_sem.at[2])
    drain(back_in, peers - 1, plain_sem.at[3])


def body(
    hidden,
    norm_gain,
    rot_left,
    rot_right,
    expert_ids,
    gate_weights,
    w_gate,
    w_up,
    w_down,
    unit_scales,
):
    n_ep, n_tp = lax.axis_size("ep"), lax.axis_size("tp")
    peers = n_ep * n_tp
    rows, width = hidden.shape
    group_rows, choices = expert_ids.shape
    held, half, ff = w_gate.shape
    experts = held * n_ep // 2
    capacity = 5 * group_rows * choices // (2 * experts)
    slots = capacity * n_ep
    plan, pieces = passes_of(held, half)
    unit_ring = min(UNIT_RING, len(pieces))
    pairs = held // plan[-1][2]
    turns = len(turns_of(pairs))
    tallest = max(deep * count for _, deep, count in plan)
    chunks, items = chunks_of(held, half)
    down_ring = min(DOWN_RING, len(items))
    broad = max(wide * count for _, wide, count in chunks)
    widest = max(wide for _, wide, _ in chunks)
    fold = SUBLANES // rows
    padded = peers * SUBLANES
    small = (
        hidden,
        norm_gain.reshape(1, width),
        rot_left,
        rot_right,
        expert_ids,
        gate_weights,
        unit_scales,
    )
    return pl.pallas_call(
        functools.partial(kernel, (n_ep, n_tp, capacity)),
        out_shape=pltpu.VMEM((rows, width), jnp.bfloat16),
        in_specs=[pl.BlockSpec(memory_space=pltpu.HBM)] * 10,
        out_specs=pl.BlockSpec(memory_space=pltpu.VMEM),
        scratch_shapes=[pltpu.VMEM(x.shape, x.dtype) for x in small]
        + [
            pltpu.VMEM((unit_ring, tallest, 2 * ff), jnp.bfloat16),
            pltpu.VMEM((down_ring, ff, broad), jnp.bfloat16),
            pltpu.VMEM((n_tp, SUBLANES, half // fold), jnp.bfloat16),
            pltpu.VMEM((peers, SUBLANES, half // fold), jnp.bfloat16),
            pltpu.VMEM((group_rows, capacity * experts), jnp.bfloat16),
            pltpu.VMEM((n_ep, group_rows, capacity * experts), jnp.bfloat16),
            pltpu.VMEM((capacity * experts, padded), jnp.float32),
            pltpu.VMEM((held, slots, half), jnp.bfloat16),
            pltpu.VMEM((held, slots, 2 * ff), jnp.float32),
            pltpu.VMEM((held, slots, 2 * ff), jnp.float32),
            pltpu.VMEM((held, slots, ff), jnp.bfloat16),
            pltpu.VMEM((fold, padded, held * slots), jnp.bfloat16),
            pltpu.VMEM((2, fold, held * slots, widest // fold), jnp.bfloat16),
            pltpu.VMEM((peers, SUBLANES, half // fold), jnp.bfloat16),
            pltpu.VMEM((peers, SUBLANES, half // fold), jnp.bfloat16),
            pltpu.SemaphoreType.DMA((max(unit_ring, len(pieces) - unit_ring + down_ring),)),
            pltpu.SemaphoreType.DMA((turns,)),
            pltpu.SemaphoreType.DMA((len(plan),)),
            pltpu.SemaphoreType.DMA((len(chunks),)),
            pltpu.SemaphoreType.DMA((6,)),
        ],
        compiler_params=pltpu.CompilerParams(
            collective_id=0, has_side_effects=True, vmem_limit_bytes=63 * 1024 * 1024
        ),
    )(*small, w_gate, w_up, w_down)


def solution(mesh):
    placed = (
        P(("groups", "ep", "tp"), None),
        P(),
        P(),
        P(),
        P(("groups", "ep"), None),
        P(("groups", "ep"), None),
        P("ep", "tp", None),
        P("ep", "tp", None),
        P("ep", None, "tp"),
        P("ep", None, None),
    )
    return jax.shard_map(
        body, mesh=mesh, in_specs=placed, out_specs=P(("groups", "ep", "tp"), None), check_vma=False
    )
```
